256 devices in a mesh: dp: 2 (over core), expert: 128 (over z, y, x).
Axes of the slice: x: 4, y: 4, z: 8, core: 2. Of those that a mesh axis runs over, the one named last changes fastest.
Arguments:
- residual: bfloat16 [16384, 4096], P(('dp', 'expert')), may hold values from -6 to 6
- attn_out: bfloat16 [16384, 4096], P(('dp', 'expert')), may hold values from -6 to 6
- norm_gain: float32 [4096], replicated, may hold values from 0.5 to 2
- routes: int32 [16384, 8], P(('dp', 'expert')), may hold values from 0 to 127, all different within a row; in each aligned block of 64 rows (0 to 63, 64 to 127, ...) at most 5 rows name the same one
- mixing: float32 [16384, 8], P(('dp', 'expert')), may hold values from 0.05 to 0.35
- gate_w: bfloat16 [128, 4096, 768], P('expert', None, 'dp'), may hold values from -0.09375 to 0.09375
- up_w: bfloat16 [128, 4096, 768], P('expert', None, 'dp'), may hold values from -0.09375 to 0.09375
- down_w: bfloat16 [128, 768, 4096], P('expert', 'dp'), may hold values from -0.21875 to 0.21875
Outputs:
- layer_out: bfloat16 [16384, 4096], P(('dp', 'expert'))
The draws below stay inside these ranges and needn't reach their ends.
Inputs may be any that keep to these rules, and one draw needn't show every extreme that they name: `routes`: each row names 8 different experts; within the rows of one device (aligned blocks of 64 rows) no expert is named by more than 5 rows.
All inputs are finite; a program needn't handle non-finite values.
Results may differ from the reference program's by a relative error of at most 0.0041.
Values may be sent and summed in bfloat16 or wider, within the bound.
No kernel may reach another device: no remote copies, remote signals or barrier semaphores. Data moves between devices by JAX's collectives and lax.ppermute only.
A program may use at most 128 MiB of HBM per device.

```python
import math
import jax
import jax.numpy as jnp
import numpy as np
from jax import lax

D = 4096
TOP = 8
FF = 768
ROWS_DEV = 64
EXPERTS = 128
TOKENS = 16384
CAP = 5


def block_scale(key, dims, split, smallest, largest):
    def one(axis_at, blocks):
        draws = jax.random.uniform(jax.random.fold_in(jax.random.fold_in(key, 6), axis_at), (blocks,), jnp.float32, smallest / len(split), largest / len(split))
        return jnp.repeat(jnp.exp(draws), dims[axis_at] // blocks).reshape((-1,) + (1,) * (len(dims) - axis_at - 1))

    factor_of = one(*split[0])
    for cut in split[1:]:
        factor_of = factor_of * one(*cut)
    return factor_of


def deal_out(key, own, number, rows, count, top, reach, slope):
    order = jax.random.permutation(key, count)
    crowded, common = load_shares(count, rows * top, reach, slope, True), load_shares(count, rows * top, reach, slope, False)
    places = jnp.arange(count)

    def named(tallies, offset_by):
        used = int((tallies > 0).sum())
        fixed = max(1, used // 4)
        passed = fixed + (places - fixed + offset_by * (used - fixed)) % max(1, count - fixed)
        return jnp.zeros((count,), jnp.int32).at[order[jnp.where(places < fixed, places, passed)]].set(jnp.asarray(tallies, jnp.int32))

    tallies = jnp.where(number % 4 == 0, named(crowded, number // 4), named(common, number - number // 4 - 1))
    mixed = jax.random.permutation(jax.random.fold_in(own, 3), count)
    giver, receiver = mixed[0:count // 2 * 2:2], mixed[1:count // 2 * 2:2]
    margin = jnp.minimum(tallies[giver] - 1, reach - tallies[receiver]) // 2
    margin = jnp.where((giver == order[0]) | (receiver == order[0]) | (tallies[receiver] == 0), 0, jnp.maximum(margin, 0))
    passed = jax.random.randint(jax.random.fold_in(own, 4), (count // 2,), 0, 1 << 20) % (margin + 1)
    tallies = tallies.at[giver].add(-passed).at[receiver].add(passed)
    members = jnp.searchsorted(jnp.cumsum(tallies), jnp.arange(rows * top), side="right").astype(jnp.int32)
    listing = members.reshape(top, rows).T
    listing = listing[jax.random.permutation(jax.random.fold_in(own, 1), rows)]
    offset_by = jax.random.randint(jax.random.fold_in(own, 2), (rows, 1), 0, top)
    return jnp.take_along_axis(listing, (jnp.arange(top)[None, :] + offset_by) % top, axis=1)


def load_shares(number_of, total, reach, slope, full):
    portions = [(1 << 20) // math.isqrt(rank ** slope) + 1 for rank in range(1, number_of + 1)]
    largest = reach if full else min(reach, max(-(-total // number_of), total * portions[0] // sum(portions)))
    least = 1 if total - largest >= number_of - 1 else 0
    counts, rest = [largest] + [least] * (number_of - 1), total - largest - least * (number_of - 1)
    while rest > 0:
        free = [i for i in range(1, number_of) if counts[i] < largest] or [i for i in range(1, number_of) if counts[i] < reach]
        whole, budget = sum([portions[i] for i in free]), rest
        for i in free:
            addition = min(reach - counts[i], max(1, budget * portions[i] // whole), rest)
            counts[i] = counts[i] + addition
            rest = rest - addition
    return np.array(counts)


def gaussian(stream_key, dims, width, most, cuts=(), held_as=jnp.bfloat16):
    gain = block_scale(stream_key, dims, cuts, -0.22, 0.18) if cuts else 1.0
    entries = jax.random.normal(stream_key, dims, jnp.float32) * width * gain
    return jnp.minimum(jnp.maximum(entries, -most), most).astype(held_as)


def setup_inputs(seed: int = 0) -> dict:
    key_of = jax.random.split(jax.random.key(seed), 9)
    residual = gaussian(key_of[0], (TOKENS, D), 1.0, 6.0, ((0, 256),))
    attn_out = gaussian(key_of[1], (TOKENS, D), 1.0, 6.0, ((0, 256),))
    norm_gain = jnp.clip(jnp.exp(jax.random.uniform(key_of[2], (D,), jnp.float32, math.log(0.5), math.log(2.0))), 0.5, 2.0)
    routes_keys = jax.random.split(jax.random.fold_in(key_of[3], 1), TOKENS // ROWS_DEV)
    routes_turns = jax.random.permutation(jax.random.fold_in(key_of[3], 3), TOKENS // ROWS_DEV)
    routes = jax.vmap(lambda own, number: deal_out(jax.random.fold_in(key_of[3], 2), own, number, ROWS_DEV, EXPERTS, TOP, CAP, 2))(routes_keys, routes_turns).reshape((TOKENS, TOP))
    mixing = jnp.clip(0.05 + 0.29999999 * jax.random.uniform(key_of[4], (TOKENS, TOP), jnp.float32) ** block_scale(key_of[4], (TOKENS, TOP), ((0, 256),), -0.2, 0.2), 0.05, 0.35)
    gate_w = gaussian(key_of[5], (EXPERTS, D, FF), D ** -0.5, 0.09375, ((0, 128), (2, 2)))
    up_w = gaussian(key_of[6], (EXPERTS, D, FF), D ** -0.5, 0.09375, ((0, 128), (2, 2)))
    down_w = gaussian(key_of[7], (EXPERTS, FF, D), FF ** -0.5, 0.21875, ((0, 128), (1, 2)))
    return {"residual": residual, "attn_out": attn_out, "norm_gain": norm_gain, "routes": routes, "mixing": mixing, "gate_w": gate_w, "up_w": up_w, "down_w": down_w}


def reference(residual, attn_out, norm_gain, routes, mixing, gate_w, up_w, down_w):
    stream = residual.astype(jnp.float32) + attn_out.astype(jnp.float32)
    square = lax.optimization_barrier(jnp.mean(stream * stream, axis=1, keepdims=True))
    normed = (stream * lax.rsqrt(square + 1e-06) * norm_gain[None, :]).astype(jnp.bfloat16)
    limit = TOKENS // ROWS_DEV * CAP

    def one_expert(total, which):
        hit = routes == which
        chosen = jnp.any(hit, axis=1)
        weight = lax.optimization_barrier(jnp.sum(jnp.where(hit, mixing, 0.0), axis=1))
        index = jnp.nonzero(chosen, size=limit, fill_value=0)[0]
        valid = (jnp.arange(limit) < jnp.sum(chosen.astype(jnp.int32))).astype(weight.dtype)
        picked = normed[index]
        gate = jnp.dot(picked, gate_w[which], preferred_element_type=jnp.float32)
        up = jnp.dot(picked, up_w[which], preferred_element_type=jnp.float32)
        hidden = (jax.nn.silu(gate) * up).astype(jnp.bfloat16)
        result = jnp.dot(hidden, down_w[which], preferred_element_type=jnp.float32).astype(jnp.bfloat16)
        share = result.astype(total.dtype) * (weight[index] * valid)[:, None]
        return (total.at[index].add(share), None)
    start = jnp.zeros(stream.shape, jnp.float32)
    total, _ = lax.scan(one_expert, start, jnp.arange(EXPERTS, dtype=jnp.int32))
    return (stream + total).astype(jnp.bfloat16)
```

```python
import jax
import jax.numpy as jnp
from jax import lax
from jax.sharding import Mesh, PartitionSpec as P

PLANE = ("y", "x")
CAP = 5
NEAR = 24
FAR = 16
OFF = 512.0


def hop(value, step):
    n = lax.axis_size("z")
    return lax.ppermute(value, "z", [(i, (i + step) % n) for i in range(n)])


def ring_gather(own):
    half = own.shape[0] // 2
    l1, r1 = hop(own, 1), hop(own, -1)
    l2, r2 = hop(l1, 1), hop(r1, -1)
    l3, r3 = hop(l2, 1), hop(r2, -1)
    ft, fb = hop(l3[:half], 1), hop(r3[half:], -1)
    return [own, l1, r1, l2, r2], [l3, r3, ft, fb]


def plane_exchange(value):
    return lax.all_to_all(value, PLANE, split_axis=0, concat_axis=0, tiled=True)


def slot_matrices(near_info, far_info, first, experts):
    info = jnp.concatenate(near_info + far_info, axis=0).astype(jnp.float32)
    n_near = sum(v.shape[0] for v in near_info)
    total = info.shape[0]
    routes, mixing = info[:, :8], info[:, 8:16]
    names = (first + jnp.arange(experts, dtype=jnp.int32)).astype(jnp.float32)
    hit = routes[:, :, None] == names[None, None, :]
    hits = jnp.any(hit, axis=1).astype(jnp.bfloat16)
    weights = jnp.sum(jnp.where(hit, mixing[:, :, None], 0.0), axis=1)
    t = jnp.arange(total, dtype=jnp.int32)
    before = (t[:, None] < t[None, :]).astype(jnp.bfloat16)
    position = lax.dot_general(hits, before, (((0,), (0,)), ((), ())), preferred_element_type=jnp.float32)
    hits_t = hits.astype(jnp.float32).T
    weights_t = weights.T
    n1 = jnp.sum(hits_t[:, :n_near], axis=1, keepdims=True)
    position = jnp.where((t < n_near)[None, :], position, position + jnp.maximum(NEAR - n1, 0.0))
    position = jnp.where(hits_t > 0, position, -1.0)

    def picks(base, size, tokens):
        want = (base + jnp.arange(size, dtype=jnp.int32)).astype(jnp.float32)
        return position[:, None, tokens] == want[None, :, None]

    def flat(pick, tokens):
        sel = pick.astype(jnp.bfloat16)
        mix = jnp.where(pick, weights_t[:, None, tokens], 0.0).astype(jnp.bfloat16)
        return sel.reshape(-1, sel.shape[-1]), mix.reshape(-1, sel.shape[-1])

    near, every = slice(0, n_near), slice(0, total)
    return flat(picks(0, NEAR, near), near), flat(picks(NEAR, FAR, every), every)


def shards(residual, attn_out, norm_gain, routes, mixing, gate_w, up_w, down_w):
    experts = lax.axis_size(PLANE)
    rows, top = routes.shape
    width = residual.shape[1]
    stream = residual.astype(jnp.float32) + attn_out.astype(jnp.float32)
    square = jnp.mean(stream * stream, axis=1, keepdims=True)
    normed = (stream * lax.rsqrt(square + 1e-06) * norm_gain[None, :]).astype(jnp.bfloat16)
    info = jnp.concatenate(
        [routes.astype(jnp.bfloat16), mixing.astype(jnp.bfloat16), jnp.zeros((rows, 128 - 2 * top), jnp.bfloat16)], axis=1
    )
    half = width // 2
    near0, far0 = ring_gather(jnp.concatenate([normed[:, :half], info], axis=1))
    near1, far1 = ring_gather(normed[:, half:])
    (s_near, w_near), (s_far, w_far) = slot_matrices(
        [v[:, half:] for v in near0], [v[:, half:] for v in far0], lax.axis_index("z") * experts, experts
    )
    near0, far0 = [v[:, :half] for v in near0], [v[:, :half] for v in far0]

    def packed(sel, blocks):
        value = jnp.dot(sel, jnp.concatenate(blocks, axis=0), preferred_element_type=jnp.float32).astype(jnp.bfloat16)
        return value.reshape(experts, -1, half)

    gate_full = lax.all_gather(gate_w, "dp", axis=2, tiled=True)[0]
    up_full = lax.all_gather(up_w, "dp", axis=2, tiled=True)[0]
    down_full = lax.all_gather(down_w, "dp", axis=1, tiled=True)[0]

    a = [plane_exchange(packed(s_near, v)) for v in (near0, near1)]
    b = [plane_exchange(packed(s_far, n + f)) for n, f in ((near0, far0), (near1, far1))]

    def hidden_of(parts):
        gate = up = 0.0
        for k, part in enumerate(parts):
            part = part.reshape(-1, half)
            at = slice(k * half, (k + 1) * half)
            gate += jnp.dot(part, gate_full[at], preferred_element_type=jnp.float32)
            up += jnp.dot(part, up_full[at], preferred_element_type=jnp.float32)
        return (jax.nn.silu(gate) * up).astype(jnp.bfloat16)

    hid_near, hid_far = hidden_of(a), hidden_of(b)

    def result(hidden, k):
        value = jnp.dot(hidden, down_full[:, k * half : (k + 1) * half], preferred_element_type=jnp.float32)
        return plane_exchange(value.astype(jnp.bfloat16).reshape(experts, -1, half)).reshape(-1, half)

    back_far = [result(hid_far, k) for k in range(2)]
    back_near = [result(hid_near, k) for k in range(2)]

    def mixed(weight, value):
        return lax.dot_general(weight, value, (((0,), (0,)), ((), ())), preferred_element_type=jnp.float32)

    n_near = 5 * rows
    outs = []
    for k in range(2):
        far = mixed(w_far[:, n_near:], back_far[k])
        h = rows // 2
        l3, r3, ft, fb = far[:rows], far[rows : 2 * rows], far[2 * rows : 2 * rows + h], far[2 * rows + h :]
        down, up = hop(ft.astype(jnp.bfloat16), -1), hop(fb.astype(jnp.bfloat16), 1)
        down = jnp.concatenate([l3[:h] + down.astype(jnp.float32), l3[h:]], axis=0)
        up = jnp.concatenate([r3[:h], r3[h:] + up.astype(jnp.float32)], axis=0)
        down, up = hop(down.astype(jnp.bfloat16), -1), hop(up.astype(jnp.bfloat16), 1)
        near = mixed(w_far[:, :n_near], back_far[k]) + mixed(w_near, back_near[k])
        own, l1, r1, l2, r2 = [near[i * rows : (i + 1) * rows] for i in range(5)]
        down, up = hop((l2 + down).astype(jnp.bfloat16), -1), hop((r2 + up).astype(jnp.bfloat16), 1)
        down, up = hop((l1 + down).astype(jnp.bfloat16), -1), hop((r1 + up).astype(jnp.bfloat16), 1)
        at = slice(k * half, (k + 1) * half)
        outs.append((stream[:, at] + (own + (down.astype(jnp.float32) + up.astype(jnp.float32)))).astype(jnp.bfloat16))
    return jnp.concatenate(outs, axis=1)


def solution(mesh):
    z, y, x = 8, 4, 4
    fine = Mesh(mesh.devices.reshape(mesh.devices.shape[0], z, y, x), ("dp", "z", "y", "x"))
    chips = ("z", "y", "x")
    return jax.shard_map(
        shards,
        mesh=fine,
        in_specs=(
            P(("dp", *chips), None),
            P(("dp", *chips), None),
            P(),
            P(("dp", *chips), None),
            P(("dp", *chips), None),
            P(chips, None, "dp"),
            P(chips, None, "dp"),
            P(chips, "dp", None),
        ),
        out_specs=P(("dp", *chips), None),
        check_vma=False,
    )
```

```python
import functools

import jax
import jax.numpy as jnp
from jax import lax
from jax.experimental import pallas as pl
from jax.experimental.pallas import tpu as pltpu
from jax.sharding import Mesh, PartitionSpec as P

PLANE = ("y", "x")
NEAR = 24
FAR = 16
OUT_WIDTHS = (1536, 2560)
BACK_WIDTHS = (1024, 3072)
TILE = 512


def hop(value, step):
    n = lax.axis_size("z")
    return lax.ppermute(value, "z", [(i, (i + step) % n) for i in range(n)])


def hops(forward, backward):
    if forward is not backward:
        forward, backward = lax.optimization_barrier((forward, backward))
    return hop(forward, 1), hop(backward, -1)


def ring_gather(own, last):
    l1, r1 = hops(own, own)
    l2, r2 = hops(l1, r1)
    l3, r3 = hops(l2, r2)
    end = hop(l3, 1) if last > 0 else hop(r3, -1)
    return [own, l1, r1, l2, r2], [l3, r3, end]


def plane_exchange(value):
    return lax.all_to_all(value, PLANE, split_axis=0, concat_axis=0, tiled=True)


def partner(value):
    return lax.ppermute(value, "dp", [(0, 1), (1, 0)])


def slot_matrices(near_info, far_info, first, experts):
    names = (first + jnp.arange(experts, dtype=jnp.int32)).astype(jnp.float32)

    def routing(infos):
        info = jnp.concatenate(infos, axis=0).astype(jnp.float32)
        hit = info[:, :8, None] == names[None, None, :]
        hits = jnp.any(hit, axis=1).astype(jnp.bfloat16)
        weights = jnp.sum(jnp.where(hit, info[:, 8:16, None], 0.0), axis=1)
        t = jnp.arange(info.shape[0], dtype=jnp.int32)
        before = (t[:, None] < t[None, :]).astype(jnp.bfloat16)
        rank = lax.dot_general(hits, before, (((0,), (0,)), ((), ())), preferred_element_type=jnp.float32)
        return hits.astype(jnp.float32).T, rank, weights.T

    def flat(position, weights, base, size):
        want = (base + jnp.arange(size, dtype=jnp.int32)).astype(jnp.float32)
        pick = position[:, None, :] == want[None, :, None]
        mix = jnp.where(pick, weights[:, None, :], 0.0).astype(jnp.bfloat16)
        tokens = pick.shape[-1]
        return pick.astype(jnp.bfloat16).reshape(-1, tokens), mix.reshape(-1, tokens)

    hits, rank, weights = routing(near_info)
    near = jnp.where(hits > 0, rank, -1.0)
    base = jnp.maximum(jnp.sum(hits, axis=1, keepdims=True), float(NEAR))
    far_hits, far_rank, far_weights = routing(far_info)
    every = jnp.concatenate([near, jnp.where(far_hits > 0, base + far_rank, -1.0)], axis=1)
    return flat(near, weights, 0, NEAR), flat(every, jnp.concatenate([weights, far_weights], axis=1), NEAR, FAR)


def dot(a, b):
    return jnp.dot(a, b, preferred_element_type=jnp.float32)


def pack_kernel(n, sel_ref, *refs):
    tokens = jnp.concatenate([b[...] for b in refs[:n]], axis=0)
    refs[-1][...] = dot(sel_ref[...], tokens).astype(refs[-1].dtype)


def pack(sel, blocks, width, total, into=None):
    slots, tokens = sel.shape
    base = 0 if into is None else (total - width) // TILE
    more = [] if into is None else [into]
    return pl.pallas_call(
        functools.partial(pack_kernel, len(blocks)),
        grid=(width // TILE,),
        out_shape=jax.ShapeDtypeStruct((slots, total), jnp.bfloat16),
        in_specs=[pl.BlockSpec((slots, tokens), lambda i: (0, 0))]
        + [pl.BlockSpec((v.shape[0], TILE), lambda i: (0, i)) for v in blocks]
        + [pl.BlockSpec(memory_space=pl.ANY)] * len(more),
        out_specs=pl.BlockSpec((slots, TILE), lambda i: (0, i + base)),
        input_output_aliases={1 + len(blocks): 0} if more else {},
        cost_estimate=pl.CostEstimate(
            flops=2 * slots * tokens * width, bytes_accessed=2 * (slots + tokens) * width, transcendentals=0
        ),
    )(sel, *blocks, *more)


def expert_kernel(n_in, n_out, *refs):
    x_refs, w_refs = refs[:n_in], refs[n_in : n_in + 6]
    out_refs = refs[n_in + 6 : n_in + 6 + n_out]
    gate_buf, up_buf, down_buf, hid_buf, sem = refs[n_in + 6 + n_out :]
    part = w_refs[0].shape[1]
    gates, ups, downs = w_refs[0:2], w_refs[2:4], w_refs[4:6]
    cuts = ((0, 256), (256, 512), (512, 768))
    groups, count = [], 0
    for low, high in cuts:
        group = []
        for sources, buf in ((gates, gate_buf), (ups, up_buf)):
            for k in range(2):
                first, last = max(low, k * part), min(high, (k + 1) * part)
                if first < last:
                    source = sources[k].at[:, first - k * part : last - k * part]
                    group.append(pltpu.make_async_copy(source, buf.at[:, first:last], sem.at[count]))
                    count += 1
        groups.append(group)
    groups.append(
        [pltpu.make_async_copy(downs[k], down_buf.at[k * part : (k + 1) * part, :], sem.at[count + k]) for k in range(2)]
    )

    def start(k):
        for c in groups[k]:
            c.start()

    def wait(k):
        for c in groups[k]:
            c.wait()

    def hidden(at):
        gate = up = None
        base = 0
        for x_ref in x_refs:
            x, n = x_ref[...], x_ref.shape[1]
            g, u = dot(x, gate_buf[base : base + n, at]), dot(x, up_buf[base : base + n, at])
            gate, up = (g, u) if gate is None else (gate + g, up + u)
            base += n
        hid_buf[:, at] = (gate / (1.0 + jnp.exp(-gate)) * up).astype(hid_buf.dtype)

    start(0)
    wait(0)
    start(1)
    start(2)
    hidden(slice(*cuts[0]))
    wait(1)
    start(3)
    hidden(slice(*cuts[1]))
    wait(2)
    hidden(slice(*cuts[2]))
    wait(3)
    base = 0
    for out_ref in out_refs:
        width = out_ref.shape[1]

        @pl.loop(0, width // TILE)
        def _(i):
            at = pl.multiple_of(i * TILE, TILE)
            value = dot(hid_buf[...], down_buf[:, pl.ds(base + at, TILE)])
            out_ref[:, pl.ds(at, TILE)] = value.astype(out_ref.dtype)

        base += width


def expert(xs, gates, ups, downs, widths):
    rows, n_in, n_out = xs[0].shape[0], len(xs), len(widths)
    depth, part = gates[0].shape
    hidden, wide = 2 * part, downs[0].shape[1]
    vmem, anywhere = pl.BlockSpec(memory_space=pltpu.VMEM), pl.BlockSpec(memory_space=pl.ANY)
    return pl.pallas_call(
        functools.partial(expert_kernel, n_in, n_out),
        out_shape=[jax.ShapeDtypeStruct((rows, w), jnp.bfloat16) for w in widths],
        in_specs=[vmem] * n_in + [anywhere] * 6,
        out_specs=[vmem] * n_out,
        scratch_shapes=[
            pltpu.VMEM((depth, hidden), jnp.bfloat16),
            pltpu.VMEM((depth, hidden), jnp.bfloat16),
            pltpu.VMEM((hidden, wide), jnp.bfloat16),
            pltpu.VMEM((rows, hidden), jnp.bfloat16),
            pltpu.SemaphoreType.DMA((10,)),
        ],
        compiler_params=pltpu.CompilerParams(vmem_limit_bytes=40 << 20),
        cost_estimate=pl.CostEstimate(
            flops=2 * rows * hidden * (2 * depth + wide),
            bytes_accessed=2 * (hidden * (2 * depth + wide) + rows * (depth + wide)),
            transcendentals=rows * hidden,
        ),
    )(*xs, *gates, *ups, *downs)


def block(residual, attn_out, norm_gain, routes, mixing, gate_w, up_w, down_w):
    experts = lax.axis_size(PLANE)
    rows, top = routes.shape
    width = residual.shape[1]
    stream = residual.astype(jnp.float32) + attn_out.astype(jnp.float32)
    square = jnp.mean(stream * stream, axis=1, keepdims=True)
    normed = (stream * lax.rsqrt(square + 1e-06) * norm_gain[None, :]).astype(jnp.bfloat16)
    info = jnp.concatenate(
        [routes.astype(jnp.bfloat16), mixing.astype(jnp.bfloat16), jnp.zeros((rows, 128 - 2 * top), jnp.bfloat16)], axis=1
    )
    w0, w1 = OUT_WIDTHS
    near0, far0 = ring_gather(jnp.concatenate([normed[:, :w0], info], axis=1), 1)
    near1, far1 = ring_gather(normed[:, w0:], -1)
    (s_near, w_near), (s_far, w_far) = slot_matrices(
        [v[:, w0:] for v in near0], [v[:, w0:] for v in far0], lax.axis_index("z") * experts, experts
    )
    gates = [gate_w[0], partner(gate_w[0])]
    ups = [up_w[0], partner(up_w[0])]
    downs = [down_w[0], partner(down_w[0])]

    a = []
    for v, w in ((near0, w0), (near1, w1)):
        value = pack(s_near, v, w, w)
        a.append(plane_exchange(value.reshape(experts, NEAR, w)).reshape(experts * NEAR, w))
    b = pack(s_far, near0 + far0, w0, width)
    b = pack(s_far, near1 + far1, w1, width, b)
    b = plane_exchange(b.reshape(experts, FAR, width)).reshape(experts * FAR, width)

    b0, _ = BACK_WIDTHS
    parts = [slice(0, b0), slice(b0, width)]
    made_near = expert(a, gates, ups, downs, BACK_WIDTHS)
    (made_far,) = expert([b], gates, ups, downs, (width,))
    back_far = plane_exchange(made_far.reshape(experts, FAR, width)).reshape(-1, width)
    back_near = {}
    for k in (1, 0):
        back_near[k] = plane_exchange(made_near[k].reshape(experts, NEAR, -1)).reshape(experts * NEAR, -1)

    def mixed(weight, value):
        return lax.dot_general(weight, value, (((0,), (0,)), ((), ())), preferred_element_type=jnp.float32)

    n_near = 5 * rows
    half = width // 2
    far = mixed(w_far[:, n_near:], back_far)
    l3, r3, end = far[:rows], far[rows : 2 * rows], far[2 * rows :].astype(jnp.bfloat16)
    up, down = hops(end[:, half:], end[:, :half])
    down = l3 + jnp.pad(down.astype(jnp.float32), ((0, 0), (0, half)))
    up = r3 + jnp.pad(up.astype(jnp.float32), ((0, 0), (half, 0)))
    far_up, far_down = hops(up.astype(jnp.bfloat16), down.astype(jnp.bfloat16))
    outs = {}
    for k in (1, 0):
        at = parts[k]
        near = mixed(w_far[:, :n_near], back_far[:, at])
        near += mixed(w_near, back_near[k])
        own, l1, r1, l2, r2 = [near[i * rows : (i + 1) * rows] for i in range(5)]
        up, down = hops((r2 + far_up[:, at]).astype(jnp.bfloat16), (l2 + far_down[:, at]).astype(jnp.bfloat16))
        up, down = hops((r1 + up).astype(jnp.bfloat16), (l1 + down).astype(jnp.bfloat16))
        outs[k] = (stream[:, at] + (own + (down.astype(jnp.float32) + up.astype(jnp.float32)))).astype(jnp.bfloat16)
    return jnp.concatenate([outs[0], outs[1]], axis=1)


def solution(mesh):
    z, y, x = 8, 4, 4
    fine = Mesh(mesh.devices.reshape(mesh.devices.shape[0], z, y, x), ("dp", "z", "y", "x"))
    chips = ("z", "y", "x")
    return jax.shard_map(
        block,
        mesh=fine,
        in_specs=(
            P(("dp", *chips), None),
            P(("dp", *chips), None),
            P(),
            P(("dp", *chips), None),
            P(("dp", *chips), None),
            P(chips, None, "dp"),
            P(chips, None, "dp"),
            P(chips, "dp", None),
        ),
        out_specs=P(("dp", *chips), None),
        check_vma=False,
    )
```

```python
import functools

import jax
import jax.numpy as jnp
from jax import lax
from jax.experimental import pallas as pl
from jax.experimental.pallas import tpu as pltpu
from jax.sharding import Mesh, PartitionSpec as P

PLANE = ("y", "x")
NEAR = 24
FAR = 16
OUT_WIDTHS = (1536, 2560)
BACK_WIDTHS = (1024, 3072)
TILE = 512


def hop(value, step):
    n = lax.axis_size("z")
    return lax.ppermute(value, "z", [(i, (i + step) % n) for i in range(n)])


def hops(forward, backward):
    if forward is not backward:
        forward, backward = lax.optimization_barrier((forward, backward))
    return hop(forward, 1), hop(backward, -1)


def ring_gather(own, last):
    l1, r1 = hops(own, own)
    l2, r2 = hops(l1, r1)
    l3, r3 = hops(l2, r2)
    end = hop(l3, 1) if last > 0 else hop(r3, -1)
    return [own, l1, r1, l2, r2], [l3, r3, end]


def plane_exchange(value):
    return lax.all_to_all(value, PLANE, split_axis=0, concat_axis=0, tiled=True)


def partner(value):
    return lax.ppermute(value, "dp", [(0, 1), (1, 0)])


def slot_matrices(near_info, far_info, first, experts):
    names = (first + jnp.arange(experts, dtype=jnp.int32)).astype(jnp.float32)

    def routing(infos):
        info = jnp.concatenate(infos, axis=0).astype(jnp.float32)
        hit = info[:, :8, None] == names[None, None, :]
        hits = jnp.any(hit, axis=1).astype(jnp.bfloat16)
        weights = jnp.sum(jnp.where(hit, info[:, 8:16, None], 0.0), axis=1)
        t = jnp.arange(info.shape[0], dtype=jnp.int32)
        before = (t[:, None] < t[None, :]).astype(jnp.bfloat16)
        rank = lax.dot_general(hits, before, (((0,), (0,)), ((), ())), preferred_element_type=jnp.float32)
        return hits.astype(jnp.float32).T, rank, weights.T

    def flat(position, weights, base, size):
        want = (base + jnp.arange(size, dtype=jnp.int32)).astype(jnp.float32)
        pick = position[:, None, :] == want[None, :, None]
        mix = jnp.where(pick, weights[:, None, :], 0.0).astype(jnp.bfloat16)
        tokens = pick.shape[-1]
        return pick.astype(jnp.bfloat16).reshape(-1, tokens), mix.reshape(-1, tokens)

    hits, rank, weights = routing(near_info)
    near = jnp.where(hits > 0, rank, -1.0)
    base = jnp.maximum(jnp.sum(hits, axis=1, keepdims=True), float(NEAR))
    far_hits, far_rank, far_weights = routing(far_info)
    every = jnp.concatenate([near, jnp.where(far_hits > 0, base + far_rank, -1.0)], axis=1)
    return flat(near, weights, 0, NEAR), flat(every, jnp.concatenate([weights, far_weights], axis=1), NEAR, FAR)


def dot(a, b):
    return jnp.dot(a, b, preferred_element_type=jnp.float32)


def pack_kernel(n, sel_ref, *refs):
    tokens = jnp.concatenate([b[...] for b in refs[:n]], axis=0)
    refs[-1][...] = dot(sel_ref[...], tokens).astype(refs[-1].dtype)


def pack(sel, blocks, width, total, into=None):
    slots, tokens = sel.shape
    tile = width // 2 if into is None else TILE
    base = 0 if into is None else (total - width) // tile
    more = [] if into is None else [into]
    return pl.pallas_call(
        functools.partial(pack_kernel, len(blocks)),
        grid=(width // tile,),
        out_shape=jax.ShapeDtypeStruct((slots, total), jnp.bfloat16),
        in_specs=[pl.BlockSpec((slots, tokens), lambda i: (0, 0))]
        + [pl.BlockSpec((v.shape[0], tile), lambda i: (0, i)) for v in blocks]
        + [pl.BlockSpec(memory_space=pl.ANY)] * len(more),
        out_specs=pl.BlockSpec((slots, tile), lambda i: (0, i + base)),
        input_output_aliases={1 + len(blocks): 0} if more else {},
        cost_estimate=pl.CostEstimate(
            flops=2 * slots * tokens * width, bytes_accessed=2 * (slots + tokens) * width, transcendentals=0
        ),
    )(sel, *blocks, *more)


def expert_kernel(n_in, n_out, *refs):
    x_refs, w_refs = refs[:n_in], refs[n_in : n_in + 6]
    out_refs = refs[n_in + 6 : n_in + 6 + n_out]
    gate_buf, up_buf, down_buf, hid_buf, sem = refs[n_in + 6 + n_out :]
    part = w_refs[0].shape[1]
    gates, ups, downs = w_refs[0:2], w_refs[2:4], w_refs[4:6]
    cuts = ((0, 256), (256, 512), (512, 768))
    groups, count = [], 0
    for low, high in cuts:
        group = []
        for sources, buf in ((gates, gate_buf), (ups, up_buf)):
            for k in range(2):
                first, last = max(low, k * part), min(high, (k + 1) * part)
                if first < last:
                    source = sources[k].at[:, first - k * part : last - k * part]
                    group.append(pltpu.make_async_copy(source, buf.at[:, first:last], sem.at[count]))
                    count += 1
        groups.append(group)
    groups.append(
        [pltpu.make_async_copy(downs[k], down_buf.at[k * part : (k + 1) * part, :], sem.at[count + k]) for k in range(2)]
    )

    def start(k):
        for c in groups[k]:
            c.start()

    def wait(k):
        for c in groups[k]:
            c.wait()

    def hidden(at):
        gate = up = None
        base = 0
        for x_ref in x_refs:
            x, n = x_ref[...], x_ref.shape[1]
            g, u = dot(x, gate_buf[base : base + n, at]), dot(x, up_buf[base : base + n, at])
            gate, up = (g, u) if gate is None else (gate + g, up + u)
            base += n
        hid_buf[:, at] = (gate / (1.0 + jnp.exp(-gate)) * up).astype(hid_buf.dtype)

    start(0)
    wait(0)
    start(1)
    start(2)
    hidden(slice(*cuts[0]))
    wait(1)
    start(3)
    hidden(slice(*cuts[1]))
    wait(2)
    hidden(slice(*cuts[2]))
    wait(3)
    base = 0
    for out_ref in out_refs:
        width = out_ref.shape[1]

        @pl.loop(0, width // TILE)
        def _(i):
            at = pl.multiple_of(i * TILE, TILE)
            value = dot(hid_buf[...], down_buf[:, pl.ds(base + at, TILE)])
            out_ref[:, pl.ds(at, TILE)] = value.astype(out_ref.dtype)

        base += width


def expert(xs, gates, ups, downs, widths):
    rows, n_in, n_out = xs[0].shape[0], len(xs), len(widths)
    depth, part = gates[0].shape
    hidden, wide = 2 * part, downs[0].shape[1]
    vmem, anywhere = pl.BlockSpec(memory_space=pltpu.VMEM), pl.BlockSpec(memory_space=pl.ANY)
    return pl.pallas_call(
        functools.partial(expert_kernel, n_in, n_out),
        out_shape=[jax.ShapeDtypeStruct((rows, w), jnp.bfloat16) for w in widths],
        in_specs=[vmem] * n_in + [anywhere] * 6,
        out_specs=[vmem] * n_out,
        scratch_shapes=[
            pltpu.VMEM((depth, hidden), jnp.bfloat16),
            pltpu.VMEM((depth, hidden), jnp.bfloat16),
            pltpu.VMEM((hidden, wide), jnp.bfloat16),
            pltpu.VMEM((rows, hidden), jnp.bfloat16),
            pltpu.SemaphoreType.DMA((10,)),
        ],
        compiler_params=pltpu.CompilerParams(vmem_limit_bytes=40 << 20),
        cost_estimate=pl.CostEstimate(
            flops=2 * rows * hidden * (2 * depth + wide),
            bytes_accessed=2 * (hidden * (2 * depth + wide) + rows * (depth + wide)),
            transcendentals=rows * hidden,
        ),
    )(*xs, *gates, *ups, *downs)


def block(residual, attn_out, norm_gain, routes, mixing, gate_w, up_w, down_w):
    experts = lax.axis_size(PLANE)
    rows, top = routes.shape
    width = residual.shape[1]
    stream = residual.astype(jnp.float32) + attn_out.astype(jnp.float32)
    square = jnp.mean(stream * stream, axis=1, keepdims=True)
    normed = (stream * lax.rsqrt(square + 1e-06) * norm_gain[None, :]).astype(jnp.bfloat16)
    info = jnp.concatenate(
        [routes.astype(jnp.bfloat16), mixing.astype(jnp.bfloat16), jnp.zeros((rows, 128 - 2 * top), jnp.bfloat16)], axis=1
    )
    w0, w1 = OUT_WIDTHS
    near0, far0 = ring_gather(jnp.concatenate([normed[:, :w0], info], axis=1), 1)
    near1, far1 = ring_gather(normed[:, w0:], -1)
    (s_near, w_near), (s_far, w_far) = slot_matrices(
        [v[:, w0:] for v in near0], [v[:, w0:] for v in far0], lax.axis_index("z") * experts, experts
    )
    gates = [gate_w[0], partner(gate_w[0])]
    ups = [up_w[0], partner(up_w[0])]
    downs = [down_w[0], partner(down_w[0])]

    a = []
    for v, w in ((near0, w0), (near1, w1)):
        value = pack(s_near, v, w, w)
        a.append(plane_exchange(value.reshape(experts, NEAR, w)).reshape(experts * NEAR, w))
    b = pack(s_far, near0 + far0, w0, width)
    b = pack(s_far, near1 + far1, w1, width, b)
    b = plane_exchange(b.reshape(experts, FAR, width)).reshape(experts * FAR, width)

    b0, _ = BACK_WIDTHS
    parts = [slice(0, b0), slice(b0, width)]
    made_near = expert(a, gates, ups, downs, BACK_WIDTHS)
    (made_far,) = expert([b], gates, ups, downs, (width,))
    back_far = plane_exchange(made_far.reshape(experts, FAR, width)).reshape(-1, width)
    back_near = {}
    for k in (1, 0):
        back_near[k] = plane_exchange(made_near[k].reshape(experts, NEAR, -1)).reshape(experts * NEAR, -1)

    def mixed(weight, value):
        return lax.dot_general(weight, value, (((0,), (0,)), ((), ())), preferred_element_type=jnp.float32)

    n_near = 5 * rows
    half = width // 2
    far = mixed(w_far[:, n_near:], back_far)
    l3, r3, end = far[:rows], far[rows : 2 * rows], far[2 * rows :].astype(jnp.bfloat16)
    up, down = hops(end[:, half:], end[:, :half])
    over = mixed(w_far[:, :n_near], back_far)
    up, down, over = lax.optimization_barrier((up, down, over))
    down = l3 + jnp.pad(down.astype(jnp.float32), ((0, 0), (0, half)))
    up = r3 + jnp.pad(up.astype(jnp.float32), ((0, 0), (half, 0)))
    far_up, far_down = hops(up.astype(jnp.bfloat16), down.astype(jnp.bfloat16))
    outs = {}
    for k in (1, 0):
        at = parts[k]
        sent = mixed(w_near[:, 3 * rows :], back_near[k]) + over[3 * rows :, at]
        kept = mixed(w_near[:, : 3 * rows], back_near[k]) + over[: 3 * rows, at]
        l2, r2 = sent[:rows], sent[rows:]
        own, l1, r1 = [kept[i * rows : (i + 1) * rows] for i in range(3)]
        up, down = hops((r2 + far_up[:, at]).astype(jnp.bfloat16), (l2 + far_down[:, at]).astype(jnp.bfloat16))
        up, down = hops((r1 + up).astype(jnp.bfloat16), (l1 + down).astype(jnp.bfloat16))
        outs[k] = (stream[:, at] + (own + (down.astype(jnp.float32) + up.astype(jnp.float32)))).astype(jnp.bfloat16)
    return jnp.concatenate([outs[0], outs[1]], axis=1)


def solution(mesh):
    z, y, x = 8, 4, 4
    fine = Mesh(mesh.devices.reshape(mesh.devices.shape[0], z, y, x), ("dp", "z", "y", "x"))
    chips = ("z", "y", "x")
    return jax.shard_map(
        block,
        mesh=fine,
        in_specs=(
            P(("dp", *chips), None),
            P(("dp", *chips), None),
            P(),
            P(("dp", *chips), None),
            P(("dp", *chips), None),
            P(chips, None, "dp"),
            P(chips, None, "dp"),
            P(chips, "dp", None),
        ),
        out_specs=P(("dp", *chips), None),
        check_vma=False,
    )
```
